256 devices in a mesh: sec: 16 (over y, z_hi), dev: 16 (over x, z_lo, core).
Axes of the slice: x: 4, y: 4, z: 8 (z_hi: 4, z_lo: 2; z = z_hi * 2 + z_lo), core: 2. Of those that a mesh axis runs over, the one named last changes fastest.
Arguments:
- velocity: bfloat16 [2, 3, 128, 192, 192], P(None, None, 'sec', 'dev'), may hold values from -6 to 6
- acoustic: float32 [4, 16, 64, 8, 512], P(None, 'sec', 'dev'), may hold values from -6 to 6
- interp: bfloat16 [512, 512], replicated, may hold values from -0.25 to 0.25
- source_peer: int32 [6144, 1], P(('sec', 'dev')), may hold values from 0 to 15; in each aligned block of 24 rows (0 to 23, 24 to 47, ...) at most 3 rows name the same one
- source_block: int32 [6144], P(('sec', 'dev')), may hold values from 0 to 35
- source_element: int32 [6144], P(('sec', 'dev')), may hold values from 0 to 31, as said below
Outputs:
- acoustic_next: float32 [4, 16, 64, 8, 512], P(None, 'sec', 'dev')
- sources: bfloat16 [6144, 2, 3, 512], P(('sec', 'dev'))
The draws below stay inside these ranges and needn't reach their ends.
Inputs may be any that keep to these rules, and one draw needn't show every extreme that they name: `source_peer`: among the rows of one device no value appears more than 3 times, and some device reaches 3. `source_element`: the 24 entries of one device are distinct.
All inputs are finite; a program needn't handle non-finite values.
Results may differ from the reference program's by a relative error of at most 0.0049.
Values may be sent and summed in bfloat16 or wider, within the bound.
A program may use at most 128 MiB of HBM per device.

```python
import math
import jax
import jax.numpy as jnp
import numpy as np
from jax import lax

CX = 8
CY = 12
FZ = 192
EX = 1
EY = 4
EZ = 8
SRC_DEV = 24
NODES = 512
STEPS = 2
FX = 128
FY = 192
GEX = 16
GEY = 64
ELEM_DEV = 32
NBLK = 36
SOURCES = 6144
CAP = 3
N_SEC = 16
N_DEV = 16


def draw_source_element(key, part):
    key_list = jax.random.split(key, SOURCES // SRC_DEV)

    def one_device(sub_key):
        return jax.random.permutation(sub_key, EX * EY * EZ)[:SRC_DEV]
    return jax.vmap(one_device)(key_list).reshape(SOURCES).astype(jnp.int32)


def set_ends(array, stream_key, smallest, top_value):
    longest = array.shape.index(max(array.shape))
    spots = []
    for shift in (0, 1):
        where = [jax.random.randint(jax.random.fold_in(stream_key, axis), (), 0, length) for axis, length in enumerate(array.shape)]
        where[longest] = (where[longest] + shift) % array.shape[longest]
        spots.append(tuple(where))
    return array.at[spots[0]].set(smallest).at[spots[1]].set(top_value)


def levels(stream_key, shape, pieces, smallest, top_value):
    loudness = 1.0
    for position, blocks in pieces:
        heights = jax.random.uniform(jax.random.fold_in(jax.random.fold_in(stream_key, 6), position), (blocks,), jnp.float32, smallest / len(pieces), top_value / len(pieces))
        loudness = loudness * jnp.repeat(jnp.exp(heights), shape[position] // blocks).reshape((-1,) + (1,) * (len(shape) - 1 - position))
    return loudness


def assign_block(key, own, number, rows, amount, top, limit, slope):
    sequence = jax.random.permutation(key, amount)
    crowded, usual = load_shares(amount, rows * top, limit, slope, True), load_shares(amount, rows * top, limit, slope, False)
    places = jnp.arange(amount)

    def named(lengths, turn):
        used = int((lengths > 0).sum())
        fixed = max(1, used // 4)
        passed = fixed + (places - fixed + turn * (used - fixed)) % max(1, amount - fixed)
        return jnp.zeros((amount,), jnp.int32).at[sequence[jnp.where(places < fixed, places, passed)]].set(jnp.asarray(lengths, jnp.int32))

    lengths = jnp.where(number % 4 == 0, named(crowded, number // 4), named(usual, number - number // 4 - 1))
    mixed = jax.random.permutation(jax.random.fold_in(own, 3), amount)
    donor, taker = mixed[0:amount // 2 * 2:2], mixed[1:amount // 2 * 2:2]
    room = jnp.minimum(lengths[donor] - 1, limit - lengths[taker]) // 2
    room = jnp.where((donor == sequence[0]) | (taker == sequence[0]) | (lengths[taker] == 0), 0, jnp.maximum(room, 0))
    passed = jax.random.randint(jax.random.fold_in(own, 4), (amount // 2,), 0, 1 << 20) % (room + 1)
    lengths = lengths.at[donor].add(-passed).at[taker].add(passed)
    labels = jnp.searchsorted(jnp.cumsum(lengths), jnp.arange(rows * top), side="right").astype(jnp.int32)
    table = labels.reshape(top, rows).T
    table = table[jax.random.permutation(jax.random.fold_in(own, 1), rows)]
    turn = jax.random.randint(jax.random.fold_in(own, 2), (rows, 1), 0, top)
    return jnp.take_along_axis(table, (jnp.arange(top)[None, :] + turn) % top, axis=1)


def load_shares(number_of, total, bound, slope, full):
    weights = [(1 << 20) // math.isqrt(grade ** slope) + 1 for grade in range(1, number_of + 1)]
    largest = bound if full else min(bound, max(-(-total // number_of), total * weights[0] // sum(weights)))
    least = 1 if total - largest >= number_of - 1 else 0
    given, spare = [largest] + [least] * (number_of - 1), total - largest - least * (number_of - 1)
    while spare > 0:
        candidates = [i for i in range(1, number_of) if given[i] < largest] or [i for i in range(1, number_of) if given[i] < bound]
        whole, budget = sum([weights[i] for i in candidates]), spare
        for i in candidates:
            extra = min(bound - given[i], max(1, budget * weights[i] // whole), spare)
            given[i] = given[i] + extra
            spare = spare - extra
    return np.array(given)


def gaussian(stream_key, shape, spread, most, cuts=(), held_as=jnp.bfloat16):
    array = spread * jax.random.normal(stream_key, shape, jnp.float32)
    if cuts:
        array = array * levels(stream_key, shape, cuts, -0.22, 0.18)
    return jnp.clip(array, -most, most).astype(held_as)


def setup_inputs(seed: int = 0) -> dict:
    keys = jax.random.split(jax.random.key(seed), 7)
    velocity = gaussian(keys[0], (STEPS, 3, FX, FY, FZ), 1.0, 6.0, ((2, 16), (3, 16)))
    acoustic = gaussian(keys[1], (4, GEX, GEY, EZ, NODES), 1.0, 6.0, ((1, 16), (2, 16)), jnp.float32)
    interp = gaussian(keys[2], (NODES, NODES), NODES ** -0.5, 0.25)
    source_peer_keys = jax.random.split(jax.random.fold_in(keys[3], 1), SOURCES // SRC_DEV)
    source_peer_turns = jax.random.permutation(jax.random.fold_in(keys[3], 3), SOURCES // SRC_DEV)
    source_peer = jax.vmap(lambda own, number: assign_block(jax.random.fold_in(keys[3], 2), own, number, SRC_DEV, N_DEV, 1, CAP, 2))(source_peer_keys, source_peer_turns).reshape((SOURCES, 1))
    source_block = set_ends(jax.random.randint(keys[4], (SOURCES,), 0, NBLK), jax.random.fold_in(keys[4], 1), 0, NBLK - 1).astype(jnp.int32)
    source_element = draw_source_element(jax.random.fold_in(keys[6], 71), 0)
    return {"velocity": velocity, "acoustic": acoustic, "interp": interp, "source_peer": source_peer, "source_block": source_block, "source_element": source_element}


time_delta = 0.03
lift_half = 14.0


def cheb_matrix():
    points_n = 8
    nodes_at = -np.cos(np.pi * np.arange(points_n) / (points_n - 1))
    weights_at = np.ones(points_n)
    weights_at[0] = 0.5
    weights_at[-1] = 0.5
    weights_at = weights_at * (-1.0) ** np.arange(points_n)
    result_mat = np.zeros((points_n, points_n))
    for row_at in range(points_n):
        for col_at in range(points_n):
            if row_at != col_at:
                result_mat[row_at, col_at] = weights_at[col_at] / weights_at[row_at] / (nodes_at[row_at] - nodes_at[col_at])
        result_mat[row_at, row_at] = -np.sum(result_mat[row_at])
    return result_mat


def lamb_of(padded):
    padded = padded.astype(jnp.float32)
    padded = jnp.pad(padded, ((0, 0), (0, 0), (0, 0), (0, 0), (1, 1)))
    inner = padded[:, :, 1:-1, 1:-1, 1:-1]
    slope_x = (padded[:, :, 2:, 1:-1, 1:-1] - padded[:, :, :-2, 1:-1, 1:-1]) * 0.5
    slope_y = (padded[:, :, 1:-1, 2:, 1:-1] - padded[:, :, 1:-1, :-2, 1:-1]) * 0.5
    slope_z = (padded[:, :, 1:-1, 1:-1, 2:] - padded[:, :, 1:-1, 1:-1, :-2]) * 0.5
    curl_x = slope_y[:, 2] - slope_z[:, 1]
    curl_y = slope_z[:, 0] - slope_x[:, 2]
    curl_z = slope_x[:, 1] - slope_y[:, 0]
    lamb_x = curl_y * inner[:, 2] - curl_z * inner[:, 1]
    lamb_y = curl_z * inner[:, 0] - curl_x * inner[:, 2]
    lamb_z = curl_x * inner[:, 1] - curl_y * inner[:, 0]
    return jnp.stack([lamb_x, lamb_y, lamb_z], axis=1).astype(jnp.bfloat16)


def to_blocks(tile_data):
    steps_n, comps_n, size_x, size_y, size_z = tile_data.shape
    shaped = tile_data.reshape(steps_n, comps_n, size_x // 8, 8, size_y // 4, 4, size_z // 16, 16)
    shaped = shaped.transpose(2, 4, 6, 0, 1, 3, 5, 7)
    return shaped.reshape((size_x // 8) * (size_y // 4) * (size_z // 16), steps_n * comps_n * 512)


def derive_tensor(current):
    matrix = jnp.asarray(cheb_matrix(), jnp.float32)
    shaped = current.reshape(current.shape[:4] + (8, 8, 8))
    highest = lax.Precision.HIGHEST

    def along_a(values):
        return jnp.einsum('ij,...jbc->...ibc', matrix, values, precision=highest)

    def along_b(values):
        return jnp.einsum('ij,...ajc->...aic', matrix, values, precision=highest)

    def along_c(values):
        return jnp.einsum('ij,...abj->...abi', matrix, values, precision=highest)

    gradient = jnp.stack([along_a(shaped[0]), along_b(shaped[0]), along_c(shaped[0])], axis=0)
    divergence = along_a(shaped[1]) + along_b(shaped[2]) + along_c(shaped[3])
    lead = current.shape[1:4]
    return divergence.reshape(lead + (512,)), gradient.reshape((3,) + lead + (512,))


def face_slab(values, node_axis, index_at):
    slab = lax.index_in_dim(values, index_at, axis=node_axis, keepdims=False)
    return slab.reshape(slab.shape[:-2] + (64,))


def face_terms(traces, padded, elem_axis):
    size_n = traces.shape[elem_axis]
    upper = lax.slice_in_dim(padded, 2, size_n + 2, axis=elem_axis)[..., :64]
    lower = lax.slice_in_dim(padded, 0, size_n, axis=elem_axis)[..., 64:]
    press_lo = traces[0, ..., :64]
    speed_lo = traces[1, ..., :64]
    press_hi = traces[0, ..., 64:]
    speed_hi = traces[1, ..., 64:]
    jump_hi = lift_half * ((speed_hi - upper[1]) - (press_hi - upper[0]))
    jump_lo = lift_half * ((lower[1] - speed_lo) - (press_lo - lower[0]))
    return jump_lo, jump_hi


def add_face(rate_view, comp_at, node_axis, index_at, term):
    term_grid = term.reshape(term.shape[:-1] + (8, 8))
    index_tuple = (comp_at,) + (slice(None),) * (node_axis - 1) + (index_at,)
    return rate_view.at[index_tuple].add(term_grid)


def tendency(current, forcing, extenders, derive):
    size_a, size_b, size_c = current.shape[1], current.shape[2], current.shape[3]
    divergence, gradient = derive(current)
    rate_all = jnp.concatenate([-divergence[None], forcing - gradient], axis=0)
    view = current.reshape(4, size_a, size_b, size_c, 8, 8, 8)
    rate_view = rate_all.reshape(4, size_a, size_b, size_c, 8, 8, 8)
    for direction in range(3):
        node_axis = 4 + direction
        pair = jnp.stack([view[0], view[1 + direction]], axis=0)
        traces = jnp.concatenate([face_slab(pair, node_axis, 0), face_slab(pair, node_axis, 7)], axis=-1)
        padded = extenders[direction](traces)
        jump_lo, jump_hi = face_terms(traces, padded, 1 + direction)
        rate_view = add_face(rate_view, 0, node_axis, 0, jump_lo)
        rate_view = add_face(rate_view, 0, node_axis, 7, jump_hi)
        rate_view = add_face(rate_view, 1 + direction, node_axis, 0, jump_lo)
        rate_view = add_face(rate_view, 1 + direction, node_axis, 7, -jump_hi)
    return rate_view.reshape(current.shape)


def advance(current, forcing, extenders, derive):
    segment_one = current + time_delta * tendency(current, forcing, extenders, derive)
    segment_two = 0.75 * current + 0.25 * (segment_one + time_delta * tendency(segment_one, forcing, extenders, derive))
    return current * (1.0 / 3.0) + (2.0 / 3.0) * (segment_two + time_delta * tendency(segment_two, forcing, extenders, derive))


def pad_axis(values, axis_at):
    widths = [(0, 0)] * values.ndim
    widths[axis_at] = (1, 1)
    return jnp.pad(values, widths)


def reference(velocity, acoustic, interp, source_peer, source_block, source_element):
    padded = jnp.pad(velocity, ((0, 0), (0, 0), (1, 1), (1, 1), (0, 0)))
    lamb_vec = lamb_of(padded)
    steps_n = lamb_vec.shape[0]
    tile_set = lamb_vec.reshape(steps_n, 3, N_SEC, CX, N_DEV, CY, FZ).transpose(2, 4, 0, 1, 3, 5, 6)
    blocks = jax.vmap(jax.vmap(to_blocks))(tile_set)
    owner_dev = jnp.arange(SOURCES, dtype=jnp.int32) // SRC_DEV
    section = owner_dev // N_DEV
    chosen = blocks[section, source_peer[:, 0], source_block]
    sources = jnp.dot(chosen.reshape(-1, 512), interp, preferred_element_type=jnp.float32).astype(jnp.bfloat16)
    sources = sources.reshape(SOURCES, steps_n, 3, 512)
    forcing = jnp.zeros((N_SEC * N_DEV, ELEM_DEV, steps_n, 3, 512), jnp.float32)
    forcing = forcing.at[owner_dev, source_element].add(sources.astype(jnp.float32))
    forcing = forcing.reshape(N_SEC, N_DEV, EX, EY, EZ, steps_n, 3, 512).transpose(5, 6, 0, 2, 1, 3, 4, 7)
    forcing = forcing.reshape(steps_n, 3, GEX, GEY, EZ, 512)
    extenders = (lambda values: pad_axis(values, 1), lambda values: pad_axis(values, 2), lambda values: pad_axis(values, 3))
    current = acoustic
    for step_at in range(steps_n):
        current = advance(current, forcing[step_at], extenders, derive_tensor)
    return current, sources
```

```python
import functools
import jax
import jax.numpy as jnp
import ml_dtypes
import numpy as np
from jax import lax
from jax.experimental import pallas as pl
from jax.experimental.pallas import tpu as pltpu
from jax.sharding import PartitionSpec as P

MESH = pl.DeviceIdType.MESH
F32 = jnp.float32
BF16 = jnp.bfloat16
time_delta = 0.03
lift_half = 14.0
STAGE = (1.0 / 3.0, 0.5, 1.0)
CAP = 3
ROWS = 16


def cheb_matrix():
    points_n = 8
    nodes_at = -np.cos(np.pi * np.arange(points_n) / (points_n - 1))
    weights_at = np.ones(points_n)
    weights_at[0] = 0.5
    weights_at[-1] = 0.5
    weights_at = weights_at * (-1.0) ** np.arange(points_n)
    result_mat = np.zeros((points_n, points_n))
    for row_at in range(points_n):
        for col_at in range(points_n):
            if row_at != col_at:
                result_mat[row_at, col_at] = (
                    weights_at[col_at] / weights_at[row_at] / (nodes_at[row_at] - nodes_at[col_at])
                )
        result_mat[row_at, row_at] = -np.sum(result_mat[row_at])
    return result_mat


def tables():
    own = -cheb_matrix()
    own[7, 7] += lift_half
    own[0, 0] -= lift_half
    eye2, eye8 = np.eye(2), np.eye(8)
    packed = []
    for dense in (np.kron(eye2, np.kron(own, eye8)).T, np.kron(eye2, np.kron(eye8, own)).T):
        high = dense.astype(ml_dtypes.bfloat16)
        low = (dense - high.astype(np.float64)).astype(ml_dtypes.bfloat16)
        packed.append(np.block([[high, low], [high, np.zeros_like(high)]]))
    coef = np.zeros((4, 4, 2, 128), np.float32)
    for out_at in range(4):
        for in_at in range(4):
            for odd in range(2):
                coef[out_at, in_at, odd, :64] = own[2 * out_at, 2 * in_at + odd]
                coef[out_at, in_at, odd, 64:] = own[2 * out_at + 1, 2 * in_at + odd]
    return np.stack(packed).astype(ml_dtypes.bfloat16), coef.reshape(32, 128)


def roll(values, shift, axis):
    size = values.shape[axis]
    return pltpu.roll(values, shift % size, axis)


def lane_iota(shape):
    return lax.broadcasted_iota(jnp.int32, shape, len(shape) - 1)


def kernel(
    n_sec, n_dev,
    vel, ac, interp, peer, block, elem, wtab, coef,
    out_q, out_s,
    velb, acv, ip, wv, vs, lr, yhs, xhr, yhr, idx_src, idx_buf, sendb, recvb, yy_ref, forc,
    fxs, fxr, fys, fyr, dgs, dgr,
    local_sem, hx_s, hx_r, hy_s, hy_r, id_s, id_r, aa_s, aa_r, fx_s, fx_r, fy_s, fy_r, dg_s, dg_r,
):
    sec = lax.axis_index("sec")
    dev = lax.axis_index("dev")
    has_x = (sec > 0, sec < n_sec - 1)
    has_y = (dev > 0, dev < n_dev - 1)
    x_at = (sec - 1, sec + 1)
    y_at = (dev - 1, dev + 1)

    def dev_of(offset):
        return lax.rem(dev + offset + n_dev, n_dev)

    for ref in (xhr, yhr, fxr, fyr, dgr):
        ref[...] = jnp.zeros(ref.shape, ref.dtype)

    barrier = pltpu.get_barrier_semaphore()
    for side in range(2):
        @pl.when(has_x[side])
        def _():
            pl.semaphore_signal(barrier, inc=1, device_id=(x_at[side], dev), device_id_type=MESH)

    def greet(offset, carry):
        pl.semaphore_signal(barrier, inc=1, device_id=(sec, dev_of(offset)), device_id_type=MESH)
        return carry

    lax.fori_loop(1, n_dev, greet, 0)

    loads = [
        pltpu.make_async_copy(vel, velb, local_sem.at[0]),
        pltpu.make_async_copy(ac, acv, local_sem.at[1]),
        pltpu.make_async_copy(wtab, wv, local_sem.at[2]),
    ] + [pltpu.make_async_copy(interp.at[:, at], ip.at[at], local_sem.at[3 + at]) for at in range(4)]
    for load in loads:
        load.start()

    vs[...] = jnp.zeros(vs.shape, F32)
    lr[...] = jnp.zeros(lr.shape, F32)

    count = peer.shape[0]
    row_k = lax.broadcasted_iota(jnp.int32, (count, 128), 0)
    col_k = lax.broadcasted_iota(jnp.int32, (count, 128), 1)
    peer_col = peer[...].astype(F32)
    peer_row = jnp.sum(jnp.where(row_k == col_k, peer_col, 0.0), axis=0, keepdims=True)
    same = (peer_row == peer_col) & (col_k < count)
    rank_col = jnp.sum(jnp.where(same & (col_k < row_k), 1.0, 0.0), axis=1, keepdims=True)
    rank_row = jnp.sum(jnp.where(same & (row_k < col_k), 1.0, 0.0), axis=0, keepdims=True)
    lane = lane_iota((1, 128))
    idx_src[0:1, :] = jnp.where(lane < count, peer_row * CAP + rank_row, -1.0)
    idx_src[1:2, :] = jnp.zeros((1, 128), F32)
    idx_src[1:2, 0:count] = block[...].astype(F32)
    key_col = peer_col * ROWS + rank_col * CAP
    key_row = peer_row * ROWS + rank_row * CAP
    idx_buf[pl.ds(dev, 1)] = idx_src[...][None]

    loads[0].wait()
    for t in range(2):
        for side, at in ((0, 11), (1, 0)):
            for slot, comp in enumerate((0, 2)):
                yhs[t, side, slot * 8:slot * 8 + 8, :] = velb[t, comp, :, at, :]
    loads[1].wait()
    for field in range(4):
        for part in range(4):
            yy_ref[0, field, part] = acv[field, :, part * 128:(part + 1) * 128]

    def put_faces(k):
        p, u1, u2 = yy_ref.at[k, 0], yy_ref.at[k, 1], yy_ref.at[k, 2]
        fxs[k, 0] = (u1[3] + p[3]).astype(BF16)
        fxs[k, 1] = (u1[0] - p[0]).astype(BF16)
        fys[k, 0] = (u2[:, 24:32] + p[:, 24:32]).reshape(32, 128).astype(BF16)
        fys[k, 1] = (u2[:, 0:8] - p[:, 0:8]).reshape(32, 128).astype(BF16)

    def x_copy(k, way, to):
        return pltpu.make_async_remote_copy(
            fxs.at[k, way], fxr.at[k, way], fx_s.at[k, way], fx_r.at[k, way],
            device_id=(to, dev), device_id_type=MESH)

    def y_copy(k, way, to):
        return pltpu.make_async_remote_copy(
            fys.at[k, way], fyr.at[k, way], fy_s.at[k, way], fy_r.at[k, way],
            device_id=(sec, to), device_id_type=MESH)

    def send_faces(k):
        for way in range(2):
            @pl.when(has_x[1 - way])
            def _():
                x_copy(k, way, x_at[1 - way]).start()
        for way in range(2):
            @pl.when(has_y[1 - way])
            def _():
                y_copy(k, way, y_at[1 - way]).start()

    def take_faces(k):
        for way in range(2):
            @pl.when(has_y[way])
            def _():
                y_copy(k, way, y_at[way]).wait_recv()
        for way in range(2):
            @pl.when(has_x[way])
            def _():
                x_copy(k, way, x_at[way]).wait_recv()

    def diagonal(k, way, to_x, to_y):
        return pltpu.make_async_remote_copy(
            dgs.at[k - 1, way], dgr.at[k - 1, way], dg_s.at[k - 1, way], dg_r.at[k - 1, way],
            device_id=(to_x, to_y), device_id_type=MESH)

    corners = ((0, 0), (1, 0), (0, 1), (1, 1))

    def send_edges(k):
        p, u1, u2 = yy_ref.at[k, 0], yy_ref.at[k, 1], yy_ref.at[k, 2]
        for at, (way_x, way_y) in enumerate(corners):
            part = 3 if way_x == 0 else 0
            rows = slice(24, 32) if way_y == 0 else slice(0, 8)
            pp = p[part, rows]
            first = u1[part, rows] + (pp if way_x == 0 else -pp)
            second = u2[part, rows] + (pp if way_y == 0 else -pp)
            dgs[k - 1, at] = jnp.concatenate([first, second], axis=0).astype(BF16)
        for at, (way_x, way_y) in enumerate(corners):
            @pl.when(has_x[1 - way_x] & has_y[1 - way_y])
            def _():
                diagonal(k, at, x_at[1 - way_x], y_at[1 - way_y]).start()

    def take_edges(k):
        for at, (way_x, way_y) in enumerate(corners):
            @pl.when(has_x[way_x] & has_y[way_y])
            def _():
                diagonal(k, at, x_at[way_x], y_at[way_y]).wait_recv()

    def hx_copy(t, way, to):
        return pltpu.make_async_remote_copy(
            vel.at[t, 1:3, 7 if way == 0 else 0], xhr.at[t, way], hx_s.at[t, way], hx_r.at[t, way],
            device_id=(to, dev), device_id_type=MESH)

    def hy_copy(t, way, to):
        return pltpu.make_async_remote_copy(
            yhs.at[t, way], yhr.at[t, way], hy_s.at[t, way], hy_r.at[t, way],
            device_id=(sec, to), device_id_type=MESH)

    def id_copy(offset, slot, to):
        return pltpu.make_async_remote_copy(
            idx_src, idx_buf.at[slot], id_s.at[offset], id_r.at[offset],
            device_id=(sec, to), device_id_type=MESH)

    def aa_copy(t, offset, slot, to):
        return pltpu.make_async_remote_copy(
            sendb.at[t, to], recvb.at[t, slot], aa_s.at[t, offset], aa_r.at[t, offset],
            device_id=(sec, to), device_id_type=MESH)

    def each_peer(action):
        def step(offset, carry):
            action(offset)
            return carry
        lax.fori_loop(1, n_dev, step, 0)

    put_faces(0)
    greeted = n_dev - 1 + has_x[0].astype(jnp.int32) + has_x[1].astype(jnp.int32)
    pl.semaphore_wait(barrier, greeted)

    def send_halo(t):
        for way in range(2):
            @pl.when(has_x[1 - way])
            def _():
                hx_copy(t, way, x_at[1 - way]).start()
        for way in range(2):
            @pl.when(has_y[1 - way])
            def _():
                hy_copy(t, way, y_at[1 - way]).start()

    send_halo(0)
    each_peer(lambda offset: id_copy(offset, dev, dev_of(offset)).start())
    send_halo(1)
    send_faces(0)

    for t in range(2):
        vs[t, :, 1:9, 1:13, 0:192] = velb[t].astype(F32)

    loads[2].wait()
    lanes = lane_iota((1, 1, 128))
    low_half = lanes < 64
    at_b = (lanes >> 3) & 7
    at_c = lanes & 7
    part_at = lax.broadcasted_iota(jnp.int32, (4, 1, 128), 0)
    lane4 = lane_iota((4, 1, 128))
    b4, c4 = (lane4 >> 3) & 7, lane4 & 7

    def on(flag):
        return jnp.where(flag, -lift_half, 0.0)

    on_x = on(((part_at == 0) & (lane4 < 64)) | ((part_at == 3) & (lane4 >= 64)))
    on_y = on((b4 == 0) | (b4 == 7))
    on_z = on((c4 == 0) | (c4 == 7))
    on_all = on_x + on_y + on_z
    ez = lax.broadcasted_iota(jnp.int32, (1, 32, 1), 1) & 7

    def along_first(values):
        turned = roll(values, 64, 2)
        even = jnp.where(low_half, values, turned)
        odd = jnp.where(low_half, turned, values)
        parts = []
        for out_at in range(4):
            total = None
            for in_at in range(4):
                row = (out_at * 4 + in_at) * 2
                term = even[in_at] * coef[row:row + 1, :] + odd[in_at] * coef[row + 1:row + 2, :]
                total = term if total is None else total + term
            parts.append(total)
        return jnp.stack(parts)

    def along_lanes(first, second, which):
        flat = jnp.concatenate([first, second], axis=0).reshape(256, 128)
        high = flat.astype(BF16)
        rest = (flat - high.astype(F32)).astype(BF16)
        both = jnp.dot(jnp.concatenate([high, rest], axis=1), wv[which], preferred_element_type=F32)
        both = (both[:, :128] + both[:, 128:]).reshape(8, 32, 128)
        return both[:4], both[4:]

    def local_rate(k):
        p, u1, u2, u3 = (yy_ref[k, field] for field in range(4))
        dp2, du2 = along_lanes(p, u2, 0)
        dp3, du3 = along_lanes(p, u3, 1)
        r1 = along_first(p) + on_x * u1
        rp = along_first(u1) + on_all * p + du2 + du3
        r2 = dp2 + on_y * u2
        r3 = dp3 + on_z * u3
        none = jnp.zeros((4, 8, 128), F32)
        out2, back2 = u2 + p, u2 - p
        from_low = jnp.where(at_b == 0, roll(jnp.concatenate([none, out2[:, :24]], axis=1), -56, 2), 0.0)
        from_high = jnp.where(at_b == 7, roll(jnp.concatenate([back2[:, 8:], none], axis=1), 56, 2), 0.0)
        out3, back3 = u3 + p, u3 - p
        lower = roll(roll(out3, 1, 1), -7, 2)
        upper = roll(roll(back3, -1, 1), 7, 2)
        below = jnp.where((at_c == 0) & (ez > 0), lower, 0.0)
        above = jnp.where((at_c == 7) & (ez < 7), upper, 0.0)
        rp = rp + lift_half * ((from_low - from_high) + (below - above))
        r2 = r2 + lift_half * (from_low + from_high)
        r3 = r3 + lift_half * (below + above)
        return rp, r1, r2, r3

    def advance_local(k, start, force):
        scale = STAGE[k % 3] * time_delta
        rates = local_rate(k)
        for field in range(4):
            rate = rates[field]
            if force is not None and field:
                rate = rate + forc[force, field - 1]
            yy_ref[k + 1, field] = yy_ref[start, field] + scale * rate

    wide = lane_iota((8, 128))

    def between(first, last):
        return (wide >= first) & (wide < last)

    def add_neighbours(k, corrected):
        amount = STAGE[k % 3] * time_delta * lift_half
        x_low, x_high = fxr[k, 0].astype(F32), fxr[k, 1].astype(F32)
        y_low = fyr[k, 0].astype(F32).reshape(4, 8, 128)
        y_high = fyr[k, 1].astype(F32).reshape(4, 8, 128)
        if corrected:
            before = STAGE[(k - 1) % 3] * time_delta * lift_half
            edges = [dgr[k - 2, at].astype(F32) * before for at in range(4)]
            ex = [edge[0:8] for edge in edges]
            ey = [edge[8:16] for edge in edges]

            def moved(values, shift, first, last):
                return jnp.where(between(first, last), roll(values, shift, 1), 0.0)

            none = jnp.zeros((16, 128), F32)
            x_low = x_low + jnp.concatenate(
                [moved(ey[0], -56, 64, 72), none, -moved(ey[2], 56, 120, 128)], axis=0)
            x_high = x_high + jnp.concatenate(
                [-moved(ey[1], -56, 0, 8), none, moved(ey[3], 56, 56, 64)], axis=0)
            nil = jnp.zeros((8, 128), F32)
            y_low = y_low + jnp.stack(
                [moved(ex[0], 64, 56, 64), nil, nil, -moved(ex[1], 64, 120, 128)])
            y_high = y_high + jnp.stack(
                [-moved(ex[2], 64, 0, 8), nil, nil, moved(ex[3], 64, 64, 72)])
        half = lane_iota((32, 128)) < 64
        x_low = amount * jnp.where(half, roll(x_low, 64, 1), 0.0)
        x_high = amount * jnp.where(half, 0.0, roll(x_high, 64, 1))
        y_low = amount * jnp.where(at_b == 0, roll(y_low, -56, 2), 0.0)
        y_high = amount * jnp.where(at_b == 7, roll(y_high, 56, 2), 0.0)
        to = k + 1
        yy_ref[to, 0, 0] += x_low
        yy_ref[to, 1, 0] += x_low
        yy_ref[to, 0, 3] -= x_high
        yy_ref[to, 1, 3] += x_high
        yy_ref[to, 0, :, 0:8] += y_low
        yy_ref[to, 2, :, 0:8] += y_low
        yy_ref[to, 0, :, 24:32] -= y_high
        yy_ref[to, 2, :, 24:32] += y_high

    advance_local(0, 0, None)

    each_peer(lambda offset: id_copy(offset, dev_of(-offset), dev_of(-offset)).wait_recv())
    row_r = lax.broadcasted_iota(jnp.int32, (1, ROWS, 1), 1)
    slot_j = jnp.where(row_r >= 3, 1, 0) + jnp.where(row_r >= 6, 1, 0)
    comp_c = row_r - 3 * slot_j
    wanted = jnp.where(row_r < 9, CAP * dev + slot_j, -7).astype(F32)
    codes = jnp.broadcast_to(idx_buf[:, 0:1, :], (n_dev, ROWS, 128))
    names = jnp.broadcast_to(idx_buf[:, 1:2, :], (n_dev, ROWS, 128))
    found = jnp.sum(jnp.where(codes == wanted, names + 1.0, 0.0), axis=2, keepdims=True)
    name = found - 1.0
    name_y = jnp.where(name >= 12.0, 1.0, 0.0) + jnp.where(name >= 24.0, 1.0, 0.0)
    target = (name - 12.0 * name_y) * 16.0 + comp_c.astype(F32) * 3.0 + name_y
    target = jnp.where(found > 0.0, target, -1.0).reshape(n_dev * ROWS, 1)
    pick = jnp.where(lane_iota((n_dev * ROWS, 192)).astype(F32) == target, 1.0, 0.0).astype(BF16)

    in_row = lane_iota((32, n_dev * ROWS)).astype(F32)
    rows_e = lax.broadcasted_iota(jnp.int32, (32, count), 0)
    hit = rows_e == elem[...]
    key_e = jnp.sum(jnp.where(hit, key_row[:, 0:count] + 1.0, 0.0), axis=1, keepdims=True)
    place = jnp.concatenate(
        [jnp.where((in_row == key_e - 1.0 + c) & (key_e > 0.0), 1.0, 0.0) for c in range(3)],
        axis=0).astype(BF16)
    in_row_k = lane_iota((count, n_dev * ROWS)).astype(F32)
    choose = jnp.concatenate(
        [jnp.where(in_row_k == key_col + c, 1.0, 0.0) for c in range(3)], axis=0).astype(BF16)

    def swap_chunks(values):
        chunk = lane_iota((1, 1, 1, 128)) >> 4
        for bit in range(3):
            step = 1 << bit
            pairs = values.reshape(4 >> bit, 2, step, 16, 128)
            first = pairs[:, 0].reshape(4, 16, 128)
            second = pairs[:, 1].reshape(4, 16, 128)
            upper = (chunk[0] >> bit) & 1 == 1
            new_first = jnp.where(upper, roll(second, 16 * step, 2), first)
            new_second = jnp.where(upper, second, roll(first, -16 * step, 2))
            shape = (4 >> bit, 1, step, 16, 128)
            values = jnp.concatenate(
                [new_first.reshape(shape), new_second.reshape(shape)], axis=1).reshape(8, 16, 128)
        return values

    def lamb_sources(t):
        for way in range(2):
            @pl.when(has_y[way])
            def _():
                hy_copy(t, way, y_at[way]).wait_recv()
        for way in range(2):
            @pl.when(has_x[way])
            def _():
                hx_copy(t, way, x_at[way]).wait_recv()
        for way, at in ((0, 0), (1, 9)):
            vs[t, 1:3, at, 1:13, 0:192] = xhr[t, way].astype(F32)
        for way, at in ((0, 0), (1, 13)):
            for slot, comp in enumerate((0, 2)):
                vs[t, comp, 1:9, at, 0:192] = yhr[t, way, slot * 8:slot * 8 + 8, :].astype(F32)

        def cells(comp, dx, dy):
            return vs[t, comp, 1 + dx:9 + dx, 1 + dy:17 + dy, :]

        def slope_x(comp):
            return (cells(comp, 1, 0) - cells(comp, -1, 0)) * 0.5

        def slope_y(comp):
            return (cells(comp, 0, 1) - cells(comp, 0, -1)) * 0.5

        def slope_z(comp):
            here = cells(comp, 0, 0)
            return (roll(here, -1, 2) - roll(here, 1, 2)) * 0.5

        curl_x = slope_y(2) - slope_z(1)
        curl_y = slope_z(0) - slope_x(2)
        curl_z = slope_x(1) - slope_y(0)
        v_x, v_y, v_z = cells(0, 0, 0), cells(1, 0, 0), cells(2, 0, 0)
        lamb = (curl_y * v_z - curl_z * v_y, curl_z * v_x - curl_x * v_z, curl_x * v_y - curl_y * v_x)
        for comp in range(3):
            for side in range(2):
                lr[side, :, comp * 12:comp * 12 + 12, :] = lamb[comp][:, :12, side * 128:side * 128 + 128]
        columns = []
        for row in range(4):
            low = swap_chunks(lr[0, :, pl.ds(row, 16, stride=4), :])
            high = swap_chunks(lr[1, :, pl.ds(row, 16, stride=4), :])
            columns.append(jnp.concatenate([low, high[:4]], axis=0))
        cut = jnp.concatenate(columns, axis=2).reshape(192, 512).astype(BF16)
        made = jnp.dot(cut, ip[...].reshape(512, 512), preferred_element_type=F32).astype(BF16)
        sent = jnp.dot(pick, made, preferred_element_type=F32).astype(BF16)
        sendb[t] = sent.reshape(n_dev, ROWS, 512)
        recvb[t, pl.ds(dev, 1)] = sendb[t, pl.ds(dev, 1)]

    def put_forcing(t):
        table = recvb[t].reshape(n_dev * ROWS, 512)
        placed = jnp.dot(place, table, preferred_element_type=F32)
        for comp in range(3):
            for part in range(4):
                forc[t, comp, part] = placed[comp * 32:comp * 32 + 32, part * 128:part * 128 + 128]

    def put_sources(t):
        table = recvb[t].reshape(n_dev * ROWS, 512)
        chosen = jnp.dot(choose, table, preferred_element_type=F32).astype(BF16)
        for comp in range(3):
            out_s[t * 3 + comp] = chosen[comp * count:comp * count + count]

    for at in range(4):
        loads[3 + at].wait()
    lamb_sources(0)
    each_peer(lambda offset: aa_copy(0, offset, dev, dev_of(offset)).start())
    take_faces(0)
    add_neighbours(0, False)
    lamb_sources(1)
    each_peer(lambda offset: aa_copy(0, offset, dev_of(-offset), dev_of(-offset)).wait_recv())
    put_forcing(0)
    for field in range(3):
        yy_ref[1, 1 + field] += (STAGE[0] * time_delta) * forc[0, field]
    put_faces(1)
    send_faces(1)
    send_edges(1)
    each_peer(lambda offset: aa_copy(1, offset, dev, dev_of(offset)).start())

    advance_local(1, 0, 0)
    put_faces(2)
    send_faces(2)
    put_sources(0)
    take_faces(1)
    add_neighbours(1, False)
    send_edges(2)

    advance_local(2, 0, 0)
    put_faces(3)
    send_faces(3)
    take_faces(2)
    take_edges(1)
    add_neighbours(2, True)
    send_edges(3)

    each_peer(lambda offset: aa_copy(1, offset, dev_of(-offset), dev_of(-offset)).wait_recv())
    put_forcing(1)
    advance_local(3, 3, 1)
    put_faces(4)
    send_faces(4)
    put_sources(1)
    take_faces(3)
    take_edges(2)
    add_neighbours(3, True)
    send_edges(4)

    advance_local(4, 3, 1)
    put_faces(5)
    send_faces(5)
    take_faces(4)
    take_edges(3)
    add_neighbours(4, True)

    advance_local(5, 3, 1)
    take_faces(5)
    take_edges(4)
    add_neighbours(5, True)
    for field in range(4):
        for part in range(4):
            out_q[field, :, part * 128:(part + 1) * 128] = yy_ref[6, field, part]

    for t in range(2):
        for way in range(2):
            @pl.when(has_x[1 - way])
            def _():
                hx_copy(t, way, x_at[1 - way]).wait_send()

            @pl.when(has_y[1 - way])
            def _():
                hy_copy(t, way, y_at[1 - way]).wait_send()
        each_peer(lambda offset: aa_copy(t, offset, dev, dev_of(offset)).wait_send())
    each_peer(lambda offset: id_copy(offset, dev, dev_of(offset)).wait_send())
    for k in range(6):
        for way in range(2):
            @pl.when(has_x[1 - way])
            def _():
                x_copy(k, way, x_at[1 - way]).wait_send()

            @pl.when(has_y[1 - way])
            def _():
                y_copy(k, way, y_at[1 - way]).wait_send()
    for k in range(1, 5):
        for at, (way_x, way_y) in enumerate(corners):
            @pl.when(has_x[1 - way_x] & has_y[1 - way_y])
            def _():
                diagonal(k, at, x_at[1 - way_x], y_at[1 - way_y]).wait_send()


def body(n_sec, n_dev, velocity, acoustic, interp, source_peer, source_block, source_element):
    count = source_peer.shape[0]
    wtab, coef = tables()
    any_spec = pl.BlockSpec(memory_space=pltpu.HBM)
    vmem = pl.BlockSpec(memory_space=pltpu.VMEM)
    dma = pltpu.SemaphoreType.DMA
    acoustic_next, sources = pl.pallas_call(
        functools.partial(kernel, n_sec, n_dev),
        out_shape=(
            jax.ShapeDtypeStruct((4, 32, 512), F32),
            jax.ShapeDtypeStruct((6, count, 512), BF16),
        ),
        in_specs=[any_spec, any_spec, any_spec, vmem, vmem, vmem, any_spec, vmem],
        out_specs=(vmem, vmem),
        scratch_shapes=[
            pltpu.VMEM((2, 3, 8, 12, 192), BF16),
            pltpu.VMEM((4, 32, 512), F32),
            pltpu.VMEM((4, 8, 16, 512), BF16),
            pltpu.VMEM((2, 256, 256), BF16),
            pltpu.VMEM((2, 3, 10, 24, 256), F32),
            pltpu.VMEM((2, 8, 64, 128), F32),
            pltpu.VMEM((2, 2, 16, 192), BF16),
            pltpu.VMEM((2, 2, 2, 12, 192), BF16),
            pltpu.VMEM((2, 2, 16, 192), BF16),
            pltpu.VMEM((2, 128), F32),
            pltpu.VMEM((n_dev, 2, 128), F32),
            pltpu.VMEM((2, n_dev, ROWS, 512), BF16),
            pltpu.VMEM((2, n_dev, ROWS, 512), BF16),
            pltpu.VMEM((7, 4, 4, 32, 128), F32),
            pltpu.VMEM((2, 3, 4, 32, 128), F32),
            pltpu.VMEM((6, 2, 32, 128), BF16),
            pltpu.VMEM((6, 2, 32, 128), BF16),
            pltpu.VMEM((6, 2, 32, 128), BF16),
            pltpu.VMEM((6, 2, 32, 128), BF16),
            pltpu.VMEM((4, 4, 16, 128), BF16),
            pltpu.VMEM((4, 4, 16, 128), BF16),
            dma((7,)),
            dma((2, 2)), dma((2, 2)), dma((2, 2)), dma((2, 2)),
            dma((n_dev,)), dma((n_dev,)),
            dma((2, n_dev)), dma((2, n_dev)),
            dma((6, 2)), dma((6, 2)), dma((6, 2)), dma((6, 2)),
            dma((4, 4)), dma((4, 4)),
        ],
        compiler_params=pltpu.CompilerParams(
            collective_id=0, has_side_effects=True, vmem_limit_bytes=40 * 1024 * 1024),
    )(
        velocity,
        acoustic.reshape(4, 32, 512),
        interp.reshape(8, 4, 16, 512),
        source_peer,
        source_block.reshape(1, count),
        source_element.reshape(1, count),
        jnp.asarray(wtab),
        jnp.asarray(coef),
    )
    sources = sources.reshape(2, 3, count, 512).transpose(2, 0, 1, 3)
    return acoustic_next.reshape(acoustic.shape), sources


def solution(mesh):
    return jax.shard_map(
        functools.partial(body, mesh.shape["sec"], mesh.shape["dev"]),
        mesh=mesh,
        in_specs=(
            P(None, None, "sec", "dev", None),
            P(None, "sec", "dev", None, None),
            P(),
            P(("sec", "dev"), None),
            P(("sec", "dev")),
            P(("sec", "dev")),
        ),
        out_specs=(P(None, "sec", "dev", None, None), P(("sec", "dev"), None, None, None)),
        check_vma=False,
    )
```

```python
import functools
import jax
import jax.numpy as jnp
import ml_dtypes
import numpy as np
from jax import lax
from jax.experimental import pallas as pl
from jax.experimental.pallas import tpu as pltpu
from jax.sharding import PartitionSpec as P

MESH = pl.DeviceIdType.MESH
F32 = jnp.float32
BF16 = jnp.bfloat16
time_delta = 0.03
lift_half = 14.0
STAGE = (1.0 / 3.0, 0.5, 1.0)
CAP = 3
ROWS = 16


def cheb_matrix():
    points_n = 8
    nodes_at = -np.cos(np.pi * np.arange(points_n) / (points_n - 1))
    weights_at = np.ones(points_n)
    weights_at[0] = 0.5
    weights_at[-1] = 0.5
    weights_at = weights_at * (-1.0) ** np.arange(points_n)
    result_mat = np.zeros((points_n, points_n))
    for row_at in range(points_n):
        for col_at in range(points_n):
            if row_at != col_at:
                result_mat[row_at, col_at] = (
                    weights_at[col_at] / weights_at[row_at] / (nodes_at[row_at] - nodes_at[col_at])
                )
        result_mat[row_at, row_at] = -np.sum(result_mat[row_at])
    return result_mat


def tables():
    own = -cheb_matrix()
    own[7, 7] += lift_half
    own[0, 0] -= lift_half
    eye2, eye8 = np.eye(2), np.eye(8)
    packed = []
    for dense in (np.kron(eye2, np.kron(own, eye8)).T, np.kron(eye2, np.kron(eye8, own)).T):
        high = dense.astype(ml_dtypes.bfloat16)
        low = (dense - high.astype(np.float64)).astype(ml_dtypes.bfloat16)
        packed.append(np.block([[high, low], [high, np.zeros_like(high)]]))
    coef = np.zeros((4, 4, 2, 128), np.float32)
    for out_at in range(4):
        for in_at in range(4):
            for odd in range(2):
                coef[out_at, in_at, odd, :64] = own[2 * out_at, 2 * in_at + odd]
                coef[out_at, in_at, odd, 64:] = own[2 * out_at + 1, 2 * in_at + odd]
    return np.stack(packed).astype(ml_dtypes.bfloat16), coef.reshape(32, 128)


def roll(values, shift, axis):
    size = values.shape[axis]
    return pltpu.roll(values, shift % size, axis)


def lane_iota(shape):
    return lax.broadcasted_iota(jnp.int32, shape, len(shape) - 1)


def kernel(
    n_sec, n_dev,
    vel, ac, interp, peer_in, block_in, elem_in, wtab, coef_in,
    out_q, out_s,
    velb, acv, ip, wv, coef, peer, block, elem, vs, xs, lr, xhs, xhr, yhr, idx_src, idx_buf, sendb, recvb, yy_ref, forc,
    fxs, fxr, fys, fyr, dgs, dgr,
    local_sem, hx_s, hx_r, hy_s, hy_r, id_s, id_r, aa_s, aa_r, fx_s, fx_r, fy_s, fy_r, dg_s, dg_r,
):
    sec = lax.axis_index("sec")
    dev = lax.axis_index("dev")
    has_x = (sec > 0, sec < n_sec - 1)
    has_y = (dev > 0, dev < n_dev - 1)
    x_at = (sec - 1, sec + 1)
    y_at = (dev - 1, dev + 1)

    def dev_of(offset):
        return lax.rem(dev + offset + n_dev, n_dev)

    for ref in (xhr, yhr, fxr, fyr, dgr):
        ref[...] = jnp.zeros(ref.shape, ref.dtype)

    barrier = pltpu.get_barrier_semaphore()
    for side in range(2):
        @pl.when(has_x[side])
        def _():
            pl.semaphore_signal(barrier, inc=1, device_id=(x_at[side], dev), device_id_type=MESH)

    def greet(offset, carry):
        pl.semaphore_signal(barrier, inc=1, device_id=(sec, dev_of(offset)), device_id_type=MESH)
        return carry

    lax.fori_loop(1, n_dev, greet, 0)

    loads = [
        pltpu.make_async_copy(vel, velb, local_sem.at[0]),
        pltpu.make_async_copy(ac, acv, local_sem.at[1]),
        pltpu.make_async_copy(wtab, wv, local_sem.at[2]),
    ] + [pltpu.make_async_copy(interp.at[:, at], ip.at[at], local_sem.at[3 + at]) for at in range(4)] + [
        pltpu.make_async_copy(coef_in, coef, local_sem.at[7]),
        pltpu.make_async_copy(peer_in, peer, local_sem.at[8]),
        pltpu.make_async_copy(block_in, block, local_sem.at[9]),
        pltpu.make_async_copy(elem_in, elem, local_sem.at[10]),
    ]
    for at in (0, 8, 9, 10, 1, 2, 7, 3, 4, 5, 6):
        loads[at].start()

    vs[...] = jnp.zeros(vs.shape, F32)
    xs[...] = jnp.zeros(xs.shape, F32)
    lr[:, 288:512, :] = jnp.zeros((2, 224, 128), F32)

    for at in (8, 9, 10):
        loads[at].wait()
    count = peer.shape[1]
    row_k = lax.broadcasted_iota(jnp.int32, (count, 128), 0)
    col_k = lax.broadcasted_iota(jnp.int32, (count, 128), 1)
    square = (count, count)
    row_s = lax.broadcasted_iota(jnp.int32, square, 0)
    col_s = lax.broadcasted_iota(jnp.int32, square, 1)
    peer_col = jnp.sum(
        jnp.where(row_s == col_s, peer[...].astype(F32), 0.0), axis=1, keepdims=True)
    peer_row = jnp.sum(jnp.where(row_k == col_k, peer_col, 0.0), axis=0, keepdims=True)
    same = (peer_row == peer_col) & (col_k < count)
    rank_col = jnp.sum(jnp.where(same & (col_k < row_k), 1.0, 0.0), axis=1, keepdims=True)
    rank_row = jnp.sum(jnp.where(same & (row_k < col_k), 1.0, 0.0), axis=0, keepdims=True)
    lane = lane_iota((1, 128))
    idx_src[0:1, :] = jnp.where(lane < count, peer_row * CAP + rank_row, -1.0)
    idx_src[1:2, :] = jnp.zeros((1, 128), F32)
    idx_src[1:2, 0:count] = block[...].astype(F32)
    key_col = peer_col * ROWS + rank_col * CAP
    key_row = peer_row * ROWS + rank_row * CAP
    idx_buf[pl.ds(dev, 1)] = idx_src[...][None]

    loads[0].wait()
    for t in range(2):
        for comp in (1, 2):
            own = velb[t, comp].astype(F32)
            for side, at in ((0, 7), (1, 0)):
                xhs[t, side, comp - 1] = own[:, at, :].astype(BF16)
    loads[1].wait()
    for field in range(4):
        for part in range(4):
            yy_ref[0, field, part] = acv[field, :, part * 128:(part + 1) * 128]

    def put_faces(k):
        p, u1, u2 = yy_ref.at[k, 0], yy_ref.at[k, 1], yy_ref.at[k, 2]
        fxs[k, 0] = (u1[3] + p[3]).astype(BF16)
        fxs[k, 1] = (u1[0] - p[0]).astype(BF16)
        fys[k, 0] = (u2[:, 24:32] + p[:, 24:32]).reshape(32, 128).astype(BF16)
        fys[k, 1] = (u2[:, 0:8] - p[:, 0:8]).reshape(32, 128).astype(BF16)

    def x_copy(k, way, to):
        return pltpu.make_async_remote_copy(
            fxs.at[k, way], fxr.at[k, way], fx_s.at[k, way], fx_r.at[k, way],
            device_id=(to, dev), device_id_type=MESH)

    def y_copy(k, way, to):
        return pltpu.make_async_remote_copy(
            fys.at[k, way], fyr.at[k, way], fy_s.at[k, way], fy_r.at[k, way],
            device_id=(sec, to), device_id_type=MESH)

    def send_faces(k):
        for way in range(2):
            @pl.when(has_x[1 - way])
            def _():
                x_copy(k, way, x_at[1 - way]).start()
        for way in range(2):
            @pl.when(has_y[1 - way])
            def _():
                y_copy(k, way, y_at[1 - way]).start()

    def take_faces(k):
        for way in range(2):
            @pl.when(has_y[way])
            def _():
                y_copy(k, way, y_at[way]).wait_recv()
        for way in range(2):
            @pl.when(has_x[way])
            def _():
                x_copy(k, way, x_at[way]).wait_recv()

    def diagonal(k, way, to_x, to_y):
        return pltpu.make_async_remote_copy(
            dgs.at[k - 1, way], dgr.at[k - 1, way], dg_s.at[k - 1, way], dg_r.at[k - 1, way],
            device_id=(to_x, to_y), device_id_type=MESH)

    corners = ((0, 0), (1, 0), (0, 1), (1, 1))

    def send_edges(k):
        p, u1, u2 = yy_ref.at[k, 0], yy_ref.at[k, 1], yy_ref.at[k, 2]
        for at, (way_x, way_y) in enumerate(corners):
            part = 3 if way_x == 0 else 0
            rows = slice(24, 32) if way_y == 0 else slice(0, 8)
            pp = p[part, rows]
            first = u1[part, rows] + (pp if way_x == 0 else -pp)
            second = u2[part, rows] + (pp if way_y == 0 else -pp)
            dgs[k - 1, at] = jnp.concatenate([first, second], axis=0).astype(BF16)
        for at, (way_x, way_y) in enumerate(corners):
            @pl.when(has_x[1 - way_x] & has_y[1 - way_y])
            def _():
                diagonal(k, at, x_at[1 - way_x], y_at[1 - way_y]).start()

    def take_edges(k):
        for at, (way_x, way_y) in enumerate(corners):
            @pl.when(has_x[way_x] & has_y[way_y])
            def _():
                diagonal(k, at, x_at[way_x], y_at[way_y]).wait_recv()

    def hx_copy(t, way, to):
        return pltpu.make_async_remote_copy(
            xhs.at[t, way], xhr.at[t, way], hx_s.at[t, way], hx_r.at[t, way],
            device_id=(to, dev), device_id_type=MESH)

    def hy_copy(t, way, to):
        return pltpu.make_async_remote_copy(
            vel.at[t, :, 11 if way == 0 else 0], yhr.at[t, way], hy_s.at[t, way], hy_r.at[t, way],
            device_id=(sec, to), device_id_type=MESH)

    def id_copy(offset, slot, to):
        return pltpu.make_async_remote_copy(
            idx_src, idx_buf.at[slot], id_s.at[offset], id_r.at[offset],
            device_id=(sec, to), device_id_type=MESH)

    def aa_copy(t, offset, slot, to):
        return pltpu.make_async_remote_copy(
            sendb.at[t, to], recvb.at[t, slot], aa_s.at[t, offset], aa_r.at[t, offset],
            device_id=(sec, to), device_id_type=MESH)

    def each_peer(action):
        def step(offset, carry):
            action(offset)
            return carry
        lax.fori_loop(1, n_dev, step, 0)

    put_faces(0)
    greeted = n_dev - 1 + has_x[0].astype(jnp.int32) + has_x[1].astype(jnp.int32)
    pl.semaphore_wait(barrier, greeted)

    def send_halo(t):
        for way in range(2):
            @pl.when(has_x[1 - way])
            def _():
                hx_copy(t, way, x_at[1 - way]).start()
        for way in range(2):
            @pl.when(has_y[1 - way])
            def _():
                hy_copy(t, way, y_at[1 - way]).start()

    send_halo(0)
    each_peer(lambda offset: id_copy(offset, dev, dev_of(offset)).start())
    send_halo(1)
    send_faces(0)

    for t in range(2):
        vs[t, :, 1:13, :, 0:192] = velb[t].astype(F32)

    loads[2].wait()
    loads[7].wait()
    lanes = lane_iota((1, 1, 128))
    low_half = lanes < 64
    at_b = (lanes >> 3) & 7
    at_c = lanes & 7
    part_at = lax.broadcasted_iota(jnp.int32, (4, 1, 128), 0)
    lane4 = lane_iota((4, 1, 128))
    b4, c4 = (lane4 >> 3) & 7, lane4 & 7

    def on(flag):
        return jnp.where(flag, -lift_half, 0.0)

    on_x = on(((part_at == 0) & (lane4 < 64)) | ((part_at == 3) & (lane4 >= 64)))
    on_y = on((b4 == 0) | (b4 == 7))
    on_z = on((c4 == 0) | (c4 == 7))
    on_all = on_x + on_y + on_z
    ez = lax.broadcasted_iota(jnp.int32, (1, 32, 1), 1) & 7

    def along_first(values):
        turned = roll(values, 64, 2)
        even = jnp.where(low_half, values, turned)
        odd = jnp.where(low_half, turned, values)
        parts = []
        for out_at in range(4):
            total = None
            for in_at in range(4):
                row = (out_at * 4 + in_at) * 2
                term = even[in_at] * coef[row:row + 1, :] + odd[in_at] * coef[row + 1:row + 2, :]
                total = term if total is None else total + term
            parts.append(total)
        return jnp.stack(parts)

    def along_lanes(first, second, which):
        flat = jnp.concatenate([first, second], axis=0).reshape(256, 128)
        high = flat.astype(BF16)
        rest = (flat - high.astype(F32)).astype(BF16)
        both = jnp.dot(jnp.concatenate([high, rest], axis=1), wv[which], preferred_element_type=F32)
        both = (both[:, :128] + both[:, 128:]).reshape(8, 32, 128)
        return both[:4], both[4:]

    def local_rate(k):
        p, u1, u2, u3 = (yy_ref[k, field] for field in range(4))
        dp2, du2 = along_lanes(p, u2, 0)
        dp3, du3 = along_lanes(p, u3, 1)
        r1 = along_first(p) + on_x * u1
        rp = along_first(u1) + on_all * p + du2 + du3
        r2 = dp2 + on_y * u2
        r3 = dp3 + on_z * u3
        none = jnp.zeros((4, 8, 128), F32)
        out2, back2 = u2 + p, u2 - p
        from_low = jnp.where(at_b == 0, roll(jnp.concatenate([none, out2[:, :24]], axis=1), -56, 2), 0.0)
        from_high = jnp.where(at_b == 7, roll(jnp.concatenate([back2[:, 8:], none], axis=1), 56, 2), 0.0)
        out3, back3 = u3 + p, u3 - p
        lower = roll(roll(out3, 1, 1), -7, 2)
        upper = roll(roll(back3, -1, 1), 7, 2)
        below = jnp.where((at_c == 0) & (ez > 0), lower, 0.0)
        above = jnp.where((at_c == 7) & (ez < 7), upper, 0.0)
        rp = rp + lift_half * ((from_low - from_high) + (below - above))
        r2 = r2 + lift_half * (from_low + from_high)
        r3 = r3 + lift_half * (below + above)
        return rp, r1, r2, r3

    def advance_local(k, start, force):
        scale = STAGE[k % 3] * time_delta
        rates = local_rate(k)
        for field in range(4):
            rate = rates[field]
            if force is not None and field:
                rate = rate + forc[force, field - 1]
            yy_ref[k + 1, field] = yy_ref[start, field] + scale * rate

    wide = lane_iota((8, 128))

    def between(first, last):
        return (wide >= first) & (wide < last)

    def add_neighbours(k, corrected):
        amount = STAGE[k % 3] * time_delta * lift_half
        x_low, x_high = fxr[k, 0].astype(F32), fxr[k, 1].astype(F32)
        y_low = fyr[k, 0].astype(F32).reshape(4, 8, 128)
        y_high = fyr[k, 1].astype(F32).reshape(4, 8, 128)
        if corrected:
            before = STAGE[(k - 1) % 3] * time_delta * lift_half
            edges = [dgr[k - 2, at].astype(F32) * before for at in range(4)]
            ex = [edge[0:8] for edge in edges]
            ey = [edge[8:16] for edge in edges]

            def moved(values, shift, first, last):
                return jnp.where(between(first, last), roll(values, shift, 1), 0.0)

            none = jnp.zeros((16, 128), F32)
            x_low = x_low + jnp.concatenate(
                [moved(ey[0], -56, 64, 72), none, -moved(ey[2], 56, 120, 128)], axis=0)
            x_high = x_high + jnp.concatenate(
                [-moved(ey[1], -56, 0, 8), none, moved(ey[3], 56, 56, 64)], axis=0)
            nil = jnp.zeros((8, 128), F32)
            y_low = y_low + jnp.stack(
                [moved(ex[0], 64, 56, 64), nil, nil, -moved(ex[1], 64, 120, 128)])
            y_high = y_high + jnp.stack(
                [-moved(ex[2], 64, 0, 8), nil, nil, moved(ex[3], 64, 64, 72)])
        half = lane_iota((32, 128)) < 64
        x_low = amount * jnp.where(half, roll(x_low, 64, 1), 0.0)
        x_high = amount * jnp.where(half, 0.0, roll(x_high, 64, 1))
        y_low = amount * jnp.where(at_b == 0, roll(y_low, -56, 2), 0.0)
        y_high = amount * jnp.where(at_b == 7, roll(y_high, 56, 2), 0.0)
        to = k + 1
        yy_ref[to, 0, 0] += x_low
        yy_ref[to, 1, 0] += x_low
        yy_ref[to, 0, 3] -= x_high
        yy_ref[to, 1, 3] += x_high
        yy_ref[to, 0, :, 0:8] += y_low
        yy_ref[to, 2, :, 0:8] += y_low
        yy_ref[to, 0, :, 24:32] -= y_high
        yy_ref[to, 2, :, 24:32] += y_high

    advance_local(0, 0, None)

    each_peer(lambda offset: id_copy(offset, dev_of(-offset), dev_of(-offset)).wait_recv())
    row_r = lax.broadcasted_iota(jnp.int32, (1, ROWS, 1), 1)
    slot_j = jnp.where(row_r >= 3, 1, 0) + jnp.where(row_r >= 6, 1, 0)
    comp_c = row_r - 3 * slot_j
    wanted = jnp.where(row_r < 9, CAP * dev + slot_j, -7).astype(F32)
    codes = jnp.broadcast_to(idx_buf[:, 0:1, :], (n_dev, ROWS, 128))
    names = jnp.broadcast_to(idx_buf[:, 1:2, :], (n_dev, ROWS, 128))
    found = jnp.sum(jnp.where(codes == wanted, names + 1.0, 0.0), axis=2, keepdims=True)
    name = found - 1.0
    name_y = jnp.where(name >= 12.0, 1.0, 0.0) + jnp.where(name >= 24.0, 1.0, 0.0)
    target = (name - 12.0 * name_y) * 16.0 + comp_c.astype(F32) * 3.0 + name_y
    target = jnp.where(found > 0.0, target, -1.0).reshape(n_dev * ROWS, 1)
    pick = jnp.where(lane_iota((n_dev * ROWS, 192)).astype(F32) == target, 1.0, 0.0).astype(BF16)

    in_row = lane_iota((32, n_dev * ROWS)).astype(F32)
    rows_e = lax.broadcasted_iota(jnp.int32, (32, count), 0)
    hit = rows_e == elem[...]
    key_e = jnp.sum(jnp.where(hit, key_row[:, 0:count] + 1.0, 0.0), axis=1, keepdims=True)
    place = jnp.concatenate(
        [jnp.where((in_row == key_e - 1.0 + c) & (key_e > 0.0), 1.0, 0.0) for c in range(3)],
        axis=0).astype(BF16)
    in_row_k = lane_iota((count, n_dev * ROWS)).astype(F32)
    choose = jnp.concatenate(
        [jnp.where(in_row_k == key_col + c, 1.0, 0.0) for c in range(3)], axis=0).astype(BF16)

    def swap_chunks(values):
        chunk = lane_iota((1, 1, 1, 128)) >> 4
        for bit in range(3):
            step = 1 << bit
            pairs = values.reshape(4 >> bit, 2, step, 16, 128)
            first = pairs[:, 0].reshape(4, 16, 128)
            second = pairs[:, 1].reshape(4, 16, 128)
            upper = (chunk[0] >> bit) & 1 == 1
            new_first = jnp.where(upper, roll(second, 16 * step, 2), first)
            new_second = jnp.where(upper, second, roll(first, -16 * step, 2))
            shape = (4 >> bit, 1, step, 16, 128)
            values = jnp.concatenate(
                [new_first.reshape(shape), new_second.reshape(shape)], axis=1).reshape(8, 16, 128)
        return values

    def lamb_sources(t):
        for way in range(2):
            @pl.when(has_y[way])
            def _():
                hy_copy(t, way, y_at[way]).wait_recv()
        for way in range(2):
            @pl.when(has_x[way])
            def _():
                hx_copy(t, way, x_at[way]).wait_recv()
        for way, at in ((0, 0), (1, 7)):
            for slot in range(2):
                xs[t, way, slot, :, at, 0:192] = xhr[t, way, slot].astype(F32)
        for way, at in ((0, 0), (1, 13)):
            vs[t, :, at, :, 0:192] = yhr[t, way].astype(F32)
        x_cell = lax.broadcasted_iota(jnp.int32, (1, 8, 1), 1)

        def cells(comp, dy):
            return vs[t, comp, 1 + dy:13 + dy]

        def slope_x(comp):
            here = cells(comp, 0)
            above = jnp.where(x_cell == 7, xs[t, 1, comp - 1], roll(here, -1, 1))
            below = jnp.where(x_cell == 0, xs[t, 0, comp - 1], roll(here, 1, 1))
            return (above - below) * 0.5

        def slope_y(comp):
            return (cells(comp, 1) - cells(comp, -1)) * 0.5

        def slope_z(comp):
            here = cells(comp, 0)
            return (roll(here, -1, 2) - roll(here, 1, 2)) * 0.5

        curl_x = slope_y(2) - slope_z(1)
        curl_y = slope_z(0) - slope_x(2)
        curl_z = slope_x(1) - slope_y(0)
        v_x, v_y, v_z = cells(0, 0), cells(1, 0), cells(2, 0)
        lamb = (curl_y * v_z - curl_z * v_y, curl_z * v_x - curl_x * v_z, curl_x * v_y - curl_y * v_x)
        for comp in range(3):
            for side in range(2):
                lr[side, comp * 96:comp * 96 + 96, :] = lamb[comp][:, :, side * 128:side * 128 + 128].reshape(96, 128)
        columns = []
        for row in range(4):
            low, high = (
                swap_chunks(jnp.stack(
                    [lr[side, pl.ds(row * 8 + at, 16, stride=32), :] for at in range(8)]))
                for side in range(2))
            columns.append(jnp.concatenate([low, high[:4]], axis=0))
        cut = jnp.concatenate(columns, axis=2).reshape(192, 512).astype(BF16)
        made = jnp.dot(cut, ip[...].reshape(512, 512), preferred_element_type=F32).astype(BF16)
        sent = jnp.dot(pick, made, preferred_element_type=F32).astype(BF16)
        sendb[t] = sent.reshape(n_dev, ROWS, 512)
        recvb[t, pl.ds(dev, 1)] = sendb[t, pl.ds(dev, 1)]

    def put_forcing(t):
        table = recvb[t].reshape(n_dev * ROWS, 512)
        placed = jnp.dot(place, table, preferred_element_type=F32)
        for comp in range(3):
            for part in range(4):
                forc[t, comp, part] = placed[comp * 32:comp * 32 + 32, part * 128:part * 128 + 128]

    def put_sources():
        chosen = [
            jnp.dot(choose, recvb[t].reshape(n_dev * ROWS, 512), preferred_element_type=F32)
            for t in range(2)]
        for comp in range(3):
            rows = slice(comp * count, comp * count + count)
            out_s[:, comp] = jnp.stack([chosen[0][rows], chosen[1][rows]], axis=1).astype(BF16)

    for at in range(4):
        loads[3 + at].wait()
    lamb_sources(0)
    each_peer(lambda offset: aa_copy(0, offset, dev, dev_of(offset)).start())
    take_faces(0)
    add_neighbours(0, False)
    lamb_sources(1)
    each_peer(lambda offset: aa_copy(0, offset, dev_of(-offset), dev_of(-offset)).wait_recv())
    put_forcing(0)
    for field in range(3):
        yy_ref[1, 1 + field] += (STAGE[0] * time_delta) * forc[0, field]
    put_faces(1)
    send_faces(1)
    send_edges(1)
    each_peer(lambda offset: aa_copy(1, offset, dev, dev_of(offset)).start())

    advance_local(1, 0, 0)
    put_faces(2)
    send_faces(2)
    take_faces(1)
    add_neighbours(1, False)
    send_edges(2)

    advance_local(2, 0, 0)
    put_faces(3)
    send_faces(3)
    take_faces(2)
    take_edges(1)
    add_neighbours(2, True)
    send_edges(3)

    each_peer(lambda offset: aa_copy(1, offset, dev_of(-offset), dev_of(-offset)).wait_recv())
    put_forcing(1)
    advance_local(3, 3, 1)
    put_faces(4)
    send_faces(4)
    put_sources()
    take_faces(3)
    take_edges(2)
    add_neighbours(3, True)
    send_edges(4)

    advance_local(4, 3, 1)
    put_faces(5)
    send_faces(5)
    take_faces(4)
    take_edges(3)
    add_neighbours(4, True)

    advance_local(5, 3, 1)
    take_faces(5)
    take_edges(4)
    add_neighbours(5, True)
    for field in range(4):
        for part in range(4):
            out_q[field, :, part * 128:(part + 1) * 128] = yy_ref[6, field, part]

    for t in range(2):
        for way in range(2):
            @pl.when(has_x[1 - way])
            def _():
                hx_copy(t, way, x_at[1 - way]).wait_send()

            @pl.when(has_y[1 - way])
            def _():
                hy_copy(t, way, y_at[1 - way]).wait_send()
        each_peer(lambda offset: aa_copy(t, offset, dev, dev_of(offset)).wait_send())
    each_peer(lambda offset: id_copy(offset, dev, dev_of(offset)).wait_send())
    for k in range(6):
        for way in range(2):
            @pl.when(has_x[1 - way])
            def _():
                x_copy(k, way, x_at[1 - way]).wait_send()

            @pl.when(has_y[1 - way])
            def _():
                y_copy(k, way, y_at[1 - way]).wait_send()
    for k in range(1, 5):
        for at, (way_x, way_y) in enumerate(corners):
            @pl.when(has_x[1 - way_x] & has_y[1 - way_y])
            def _():
                diagonal(k, at, x_at[1 - way_x], y_at[1 - way_y]).wait_send()


def finish(q_in, s_in, q_out, s_out, sems):
    copies = [
        pltpu.make_async_copy(q_in, q_out, sems.at[0]),
        pltpu.make_async_copy(s_in, s_out, sems.at[1]),
    ]
    for copy in copies:
        copy.start()
    for copy in copies:
        copy.wait()


def body(n_sec, n_dev, velocity, acoustic, interp, source_peer, source_block, source_element):
    count = source_peer.shape[0]
    wtab, coef = tables()
    hbm = pl.BlockSpec(memory_space=pltpu.HBM)
    vmem = pl.BlockSpec(memory_space=pltpu.VMEM)
    dma = pltpu.SemaphoreType.DMA
    acoustic_next, sources = pl.pallas_call(
        functools.partial(kernel, n_sec, n_dev),
        out_shape=(
            pltpu.VMEM((4, 32, 512), F32),
            pltpu.VMEM((count, 3, 2, 512), BF16),
        ),
        in_specs=[hbm] * 8,
        out_specs=(vmem, vmem),
        scratch_shapes=[
            pltpu.VMEM((2, 3, 12, 8, 192), BF16),
            pltpu.VMEM((4, 32, 512), F32),
            pltpu.VMEM((4, 8, 16, 512), BF16),
            pltpu.VMEM((2, 256, 256), BF16),
            pltpu.VMEM((32, 128), F32),
            pltpu.VMEM((1, count), jnp.int32),
            pltpu.VMEM((1, count), jnp.int32),
            pltpu.VMEM((1, count), jnp.int32),
            pltpu.VMEM((2, 3, 14, 8, 256), F32),
            pltpu.VMEM((2, 2, 2, 12, 8, 256), F32),
            pltpu.VMEM((2, 512, 128), F32),
            pltpu.VMEM((2, 2, 2, 12, 192), BF16),
            pltpu.VMEM((2, 2, 2, 12, 192), BF16),
            pltpu.VMEM((2, 2, 3, 8, 192), BF16),
            pltpu.VMEM((2, 128), F32),
            pltpu.VMEM((n_dev, 2, 128), F32),
            pltpu.VMEM((2, n_dev, ROWS, 512), BF16),
            pltpu.VMEM((2, n_dev, ROWS, 512), BF16),
            pltpu.VMEM((7, 4, 4, 32, 128), F32),
            pltpu.VMEM((2, 3, 4, 32, 128), F32),
            pltpu.VMEM((6, 2, 32, 128), BF16),
            pltpu.VMEM((6, 2, 32, 128), BF16),
            pltpu.VMEM((6, 2, 32, 128), BF16),
            pltpu.VMEM((6, 2, 32, 128), BF16),
            pltpu.VMEM((4, 4, 16, 128), BF16),
            pltpu.VMEM((4, 4, 16, 128), BF16),
            dma((11,)),
            dma((2, 2)), dma((2, 2)), dma((2, 2)), dma((2, 2)),
            dma((n_dev,)), dma((n_dev,)),
            dma((2, n_dev)), dma((2, n_dev)),
            dma((6, 2)), dma((6, 2)), dma((6, 2)), dma((6, 2)),
            dma((4, 4)), dma((4, 4)),
        ],
        compiler_params=pltpu.CompilerParams(
            collective_id=0, has_side_effects=True, vmem_limit_bytes=66400000),
    )(
        velocity.transpose(0, 1, 3, 2, 4),
        acoustic.reshape(4, 32, 512),
        interp.reshape(8, 4, 16, 512),
        source_peer.reshape(1, count),
        source_block.reshape(1, count),
        source_element.reshape(1, count),
        jnp.asarray(wtab),
        jnp.asarray(coef),
    )
    acoustic_next, sources = pl.pallas_call(
        finish,
        out_shape=(
            jax.ShapeDtypeStruct((4, 32, 512), F32),
            jax.ShapeDtypeStruct((count, 3, 2, 512), BF16),
        ),
        in_specs=[vmem, vmem],
        out_specs=(hbm, hbm),
        scratch_shapes=[dma((2,))],
        compiler_params=pltpu.CompilerParams(vmem_limit_bytes=1024 * 1024),
    )(acoustic_next, sources)
    return acoustic_next.reshape(acoustic.shape), sources.transpose(0, 2, 1, 3)


def solution(mesh):
    return jax.shard_map(
        functools.partial(body, mesh.shape["sec"], mesh.shape["dev"]),
        mesh=mesh,
        in_specs=(
            P(None, None, "sec", "dev", None),
            P(None, "sec", "dev", None, None),
            P(),
            P(("sec", "dev"), None),
            P(("sec", "dev")),
            P(("sec", "dev")),
        ),
        out_specs=(P(None, "sec", "dev", None, None), P(("sec", "dev"), None, None, None)),
        check_vma=False,
    )
```
